128 devices in a mesh: attn: 16 (over z_lo, x, core), expert: 8 (over y, z_hi).
Axes of the slice: x: 4, y: 4, z: 4 (z_hi: 2, z_lo: 2; z = z_hi * 2 + z_lo), core: 2. Of those that a mesh axis runs over, the one named last changes fastest.
Arguments:
- hidden: bfloat16 [16384, 2048], P(('attn', 'expert')), may hold values from -6 to 6
- queries: bfloat16 [16384, 4096], P(('attn', 'expert')), may hold values from -6 to 6
- new_keys: bfloat16 [16384, 512], P(('attn', 'expert')), may hold values from -6 to 6
- new_values: bfloat16 [16384, 512], P(('attn', 'expert')), may hold values from -6 to 6
- cache_keys: bfloat16 [128, 4096, 512], P(('attn', 'expert')), may hold values from -6 to 6
- cache_values: bfloat16 [128, 4096, 512], P(('attn', 'expert')), may hold values from -6 to 6
- option_ids: int32 [128, 128], P(('attn', 'expert')), may hold values from 0 to 3, never falling along the last dimension, each value on 1 to 64 neighbouring positions
- prompt_lengths: int32 [128], P(('attn', 'expert')), may hold values from 1 to 4096, 393216 in all
- query_gain: float32 [128], replicated, may hold values from 0.25 to 1.75
- key_gain: float32 [128], replicated, may hold values from 0.25 to 1.75
- out_proj: bfloat16 [4096, 2048], P('expert'), may hold values from -0.09375 to 0.09375
- post_gain: float32 [2048], replicated, may hold values from 0.25 to 1.75
- route_ids: int32 [16384, 8], P(('attn', 'expert')), may hold values from 0 to 127, all different within a row; in each aligned block of 128 rows (0 to 127, 128 to 255, ...) at most 12 rows name the same one
- route_weights: float32 [16384, 8], P(('attn', 'expert')), may hold values from 0.05 to 1
- expert_gate: bfloat16 [128, 2048, 768], P(('attn', 'expert')), may hold values from -0.125 to 0.125
- expert_up: bfloat16 [128, 2048, 768], P(('attn', 'expert')), may hold values from -0.125 to 0.125
- expert_down: bfloat16 [128, 768, 2048], P(('attn', 'expert')), may hold values from -0.21875 to 0.21875
Outputs:
- layer_out: bfloat16 [16384, 2048], P(('attn', 'expert'))
The draws below stay inside these ranges and needn't reach their ends.
Inputs may be any that keep to these rules, and one draw needn't show every extreme that they name: `route_ids`: each row names 8 different experts. Among the 128 rows of one prompt (an aligned block of rows) no expert is named more than 12 times, and in every draw some expert is named exactly 12 times in some block. `option_ids`: along a prompt's 128 rows the option numbers never fall; each option holds 1 to 64 rows, and some option holds exactly 64. `prompt_lengths`: the lengths of all prompts sum to 393216, and the longest is exactly 4096.
All inputs are finite; a program needn't handle non-finite values. No bound on the sum of `prompt_lengths` on one device may be relied on, other than what follows from the above.
Results may differ from the reference program's by a relative error of at most 0.0095.
Values may be sent and summed in bfloat16 or wider, within the bound.
No kernel may reach another device: no remote copies, remote signals or barrier semaphores. Data moves between devices by JAX's collectives and lax.ppermute only.
A program may use at most 128 MiB of HBM per device.

```python
import math
import jax
import jax.numpy as jnp
import numpy as np
from jax import lax

D_MODEL = 2048
HEADS = 32
KV_HEADS = 4
HEAD_DIM = 128
EXPERT_FF = 768
TOP_K = 8
OPTIONS = 4
ANS_DEV = 128
PROMPT_LEN = 4096
EXPERTS = 128
PROMPTS = 128
ROWS = 16384
ANS_MOST = 64
CAPACITY = 12


def levels(own_key, dims, pieces, smallest, high):
    def one(dim, parts):
        draws = jax.random.uniform(jax.random.fold_in(jax.random.fold_in(own_key, 6), dim), (parts,), jnp.float32, smallest / len(pieces), high / len(pieces))
        return jnp.repeat(jnp.exp(draws), dims[dim] // parts).reshape((-1,) + (1,) * (len(dims) - dim - 1))

    level = one(*pieces[0])
    for cut in pieces[1:]:
        level = level * one(*cut)
    return level


def length_profile(number_of, total, bound, slope):
    weights = [(1 << 20) // math.isqrt(grade ** slope) + 1 for grade in range(2, number_of + 1)]
    spare, holding = total - bound - (number_of - 1), [1] * (number_of - 1)
    while spare > 0:
        movable = [i for i in range(number_of - 1) if holding[i] < bound]
        whole, budget = sum([weights[i] for i in movable]), spare
        for i in movable:
            addition = min(bound - holding[i], max(1, budget * weights[i] // whole), spare)
            holding[i] = holding[i] + addition
            spare = spare - addition
    return np.array([bound] + holding)


def ragged(own_key, amount, total, limit, skew):
    if amount == 2:
        one = jax.random.randint(own_key, (), max(1, total - limit), min(limit, total - 1) + 1)
        return jnp.stack([one, total - one])
    lengths = jnp.asarray(length_profile(amount, total, limit, skew), jnp.int32)
    couples = (amount - 1) // 2
    giver, receiver = lengths[1:1 + 2 * couples:2], lengths[2:2 + 2 * couples:2]
    room = jnp.minimum(giver - 1, limit - receiver)
    passed = jax.random.randint(jax.random.fold_in(own_key, 1), (couples,), 0, 1 << 20) % (room + 1)
    lengths = lengths.at[1:1 + 2 * couples:2].set(giver - passed).at[2:2 + 2 * couples:2].set(receiver + passed)
    return lengths[jax.random.permutation(jax.random.fold_in(own_key, 2), amount)]


def shared_out(stream_key, own, number, rows, count, top, most, lean):
    ranking = jax.random.permutation(stream_key, count)
    packed, usual = shares(count, rows * top, most, lean, True), shares(count, rows * top, most, lean, False)
    places = jnp.arange(count)

    def named(lengths, turn):
        used = int((lengths > 0).sum())
        fixed = max(1, used // 4)
        moved = fixed + (places - fixed + turn * (used - fixed)) % max(1, count - fixed)
        return jnp.zeros((count,), jnp.int32).at[ranking[jnp.where(places < fixed, places, moved)]].set(jnp.asarray(lengths, jnp.int32))

    lengths = jnp.where(number % 4 == 0, named(packed, number // 4), named(usual, number - number // 4 - 1))
    mixed = jax.random.permutation(jax.random.fold_in(own, 3), count)
    donor, receiver = mixed[0:count // 2 * 2:2], mixed[1:count // 2 * 2:2]
    margin = jnp.minimum(lengths[donor] - 1, most - lengths[receiver]) // 2
    margin = jnp.where((donor == ranking[0]) | (receiver == ranking[0]) | (lengths[receiver] == 0), 0, jnp.maximum(margin, 0))
    moved = jax.random.randint(jax.random.fold_in(own, 4), (count // 2,), 0, 1 << 20) % (margin + 1)
    lengths = lengths.at[donor].add(-moved).at[receiver].add(moved)
    members = jnp.searchsorted(jnp.cumsum(lengths), jnp.arange(rows * top), side="right").astype(jnp.int32)
    listing = members.reshape(top, rows).T
    listing = listing[jax.random.permutation(jax.random.fold_in(own, 1), rows)]
    turn = jax.random.randint(jax.random.fold_in(own, 2), (rows, 1), 0, top)
    return jnp.take_along_axis(listing, (jnp.arange(top)[None, :] + turn) % top, axis=1)


def shares(number_of, total, bound, slope, full):
    loads = [(1 << 20) // math.isqrt(grade ** slope) + 1 for grade in range(1, number_of + 1)]
    largest = bound if full else min(bound, max(-(-total // number_of), total * loads[0] // sum(loads)))
    least = 1 if total - largest >= number_of - 1 else 0
    counts, rest = [largest] + [least] * (number_of - 1), total - largest - least * (number_of - 1)
    while rest > 0:
        free = [i for i in range(1, number_of) if counts[i] < largest] or [i for i in range(1, number_of) if counts[i] < bound]
        mass, left = sum([loads[i] for i in free]), rest
        for i in free:
            addition = min(bound - counts[i], max(1, left * loads[i] // mass), rest)
            counts[i] = counts[i] + addition
            rest = rest - addition
    return np.array(counts)


def centred(stream_key, shape, spread, most, pieces=(), kind=jnp.bfloat16):
    values = jax.random.normal(stream_key, shape, jnp.float32) * spread
    if len(pieces) > 0:
        values = levels(stream_key, shape, pieces, -0.22, 0.18) * values
    return jnp.clip(values, min=-most, max=most).astype(kind)


def setup_inputs(seed: int = 0) -> dict:
    seeds = jax.random.split(jax.random.key(seed), 18)
    hidden = centred(seeds[0], (ROWS, D_MODEL), 1.0, 6.0, ((0, 128),))
    queries = centred(seeds[1], (ROWS, HEADS * HEAD_DIM), 1.0, 6.0, ((0, 128),))
    new_keys = centred(seeds[2], (ROWS, KV_HEADS * HEAD_DIM), 1.0, 6.0, ((0, 128),))
    new_values = centred(seeds[3], (ROWS, KV_HEADS * HEAD_DIM), 1.0, 6.0, ((0, 128),))
    cache_keys = centred(seeds[4], (PROMPTS, PROMPT_LEN, KV_HEADS * HEAD_DIM), 1.0, 6.0, ((0, 128),))
    cache_values = centred(seeds[5], (PROMPTS, PROMPT_LEN, KV_HEADS * HEAD_DIM), 1.0, 6.0, ((0, 128),))
    option_ids = jax.vmap(lambda own: jnp.searchsorted(jnp.cumsum(ragged(own, OPTIONS, ANS_DEV, ANS_MOST, 1)), jnp.arange(ANS_DEV), side="right"))(jax.random.split(seeds[6], PROMPTS)).reshape((PROMPTS, ANS_DEV)).astype(jnp.int32)
    prompt_lengths = ragged(seeds[7], PROMPTS, 3 * PROMPTS * PROMPT_LEN // 4, PROMPT_LEN, 2).astype(jnp.int32)
    query_gain = jnp.clip(1.0 + 0.15 * jax.random.normal(seeds[8], (HEAD_DIM,), jnp.float32), 0.25, 1.75)
    key_gain = jnp.clip(1.0 + 0.15 * jax.random.normal(seeds[9], (HEAD_DIM,), jnp.float32), 0.25, 1.75)
    out_proj = centred(seeds[10], (HEADS * HEAD_DIM, D_MODEL), (HEADS * HEAD_DIM) ** -0.5, 0.09375, ((0, 8),))
    post_gain = jnp.clip(1.0 + 0.15 * jax.random.normal(seeds[11], (D_MODEL,), jnp.float32), 0.25, 1.75)
    route_ids_keys = jax.random.split(jax.random.fold_in(seeds[12], 1), ROWS // ANS_DEV)
    route_ids_turns = jax.random.permutation(jax.random.fold_in(seeds[12], 3), ROWS // ANS_DEV)
    route_ids = jax.vmap(lambda own, number: shared_out(jax.random.fold_in(seeds[12], 2), own, number, ANS_DEV, EXPERTS, TOP_K, CAPACITY, 2))(route_ids_keys, route_ids_turns).reshape((ROWS, TOP_K))
    route_weights = jnp.clip(jnp.exp(math.log(1.0) - 2.9957323 * jax.random.uniform(seeds[13], (ROWS, TOP_K), jnp.float32) ** levels(seeds[13], (ROWS, TOP_K), ((0, 128),), -0.2, 0.2)), 0.05, 1.0)
    expert_gate = centred(seeds[14], (EXPERTS, D_MODEL, EXPERT_FF), D_MODEL ** -0.5, 0.125, ((0, 128),))
    expert_up = centred(seeds[15], (EXPERTS, D_MODEL, EXPERT_FF), D_MODEL ** -0.5, 0.125, ((0, 128),))
    expert_down = centred(seeds[16], (EXPERTS, EXPERT_FF, D_MODEL), EXPERT_FF ** -0.5, 0.21875, ((0, 128),))
    return {"hidden": hidden, "queries": queries, "new_keys": new_keys, "new_values": new_values, "cache_keys": cache_keys, "cache_values": cache_values, "option_ids": option_ids, "prompt_lengths": prompt_lengths, "query_gain": query_gain, "key_gain": key_gain, "out_proj": out_proj, "post_gain": post_gain, "route_ids": route_ids, "route_weights": route_weights, "expert_gate": expert_gate, "expert_up": expert_up, "expert_down": expert_down}


norm_eps = 1e-06

def rms_scaled(values, gain_row):
    mean_square = lax.optimization_barrier(jnp.mean(values * values, axis=-1, keepdims=True))
    return values * lax.rsqrt(mean_square + norm_eps) * gain_row

def widened_rounded_rows(values):
    return lax.optimization_barrier(values.astype(jnp.bfloat16)).astype(jnp.float32)

def attend_prompt(bundle, query_gain, key_gain):
    query_rows, incoming_keys, fresh_values, past_keys, past_values, option_row, prompt_length = bundle
    groups = HEADS // KV_HEADS
    total_keys = PROMPT_LEN + ANS_DEV
    merged_queries = rms_scaled(query_rows.astype(jnp.float32).reshape(ANS_DEV, KV_HEADS, groups, HEAD_DIM), query_gain)
    merged_queries = widened_rounded_rows(merged_queries * HEAD_DIM ** (-0.5))
    merged_keys = jnp.concatenate([past_keys, incoming_keys], axis=0).astype(jnp.float32).reshape(total_keys, KV_HEADS, HEAD_DIM)
    merged_keys = widened_rounded_rows(rms_scaled(merged_keys, key_gain))
    merged_values = jnp.concatenate([past_values, fresh_values], axis=0).astype(jnp.float32).reshape(total_keys, KV_HEADS, HEAD_DIM)
    logit_scores = jnp.einsum('nfow,pfw->nfop', merged_queries, merged_keys)
    past_live = jnp.arange(PROMPT_LEN, dtype=jnp.int32) < prompt_length
    positions = jnp.arange(ANS_DEV, dtype=jnp.int32)
    fresh_live = (option_row[:, None] == option_row[None, :]) & (positions[None, :] <= positions[:, None])
    visible = jnp.concatenate([jnp.broadcast_to(past_live[None, :], (ANS_DEV, PROMPT_LEN)), fresh_live], axis=1)
    attention_weights = jnp.where(visible[:, None, None, :], jnp.exp(logit_scores), jnp.float32(0.0))
    denominator = lax.optimization_barrier(jnp.sum(attention_weights, axis=-1))
    weighted_values = jnp.einsum('wvof,fvm->wvom', widened_rounded_rows(attention_weights), merged_values)
    return (weighted_values / denominator[..., None]).reshape(ANS_DEV, HEADS * HEAD_DIM).astype(jnp.bfloat16)

def rank_block(id_block):
    onehot = (id_block[:, None] == jnp.arange(EXPERTS, dtype=jnp.int32)[None, :]).astype(jnp.int32)
    earlier = jnp.cumsum(onehot, axis=0) - onehot
    return lax.optimization_barrier(jnp.sum(earlier * onehot, axis=1)).astype(jnp.int32)

def reference(hidden, queries, new_keys, new_values, cache_keys, cache_values, option_ids, prompt_lengths, query_gain, key_gain, out_proj, post_gain, route_ids, route_weights, expert_gate, expert_up, expert_down):

    def one_prompt(bundle):
        return attend_prompt(bundle, query_gain, key_gain)
    attended = lax.map(one_prompt, (queries.reshape(PROMPTS, ANS_DEV, HEADS * HEAD_DIM), new_keys.reshape(PROMPTS, ANS_DEV, KV_HEADS * HEAD_DIM), new_values.reshape(PROMPTS, ANS_DEV, KV_HEADS * HEAD_DIM), cache_keys, cache_values, option_ids, prompt_lengths))
    attended = attended.reshape(ROWS, HEADS * HEAD_DIM)
    projected = jnp.dot(attended, out_proj, preferred_element_type=jnp.float32)
    residual = (hidden.astype(jnp.float32) + projected).astype(jnp.bfloat16)
    normed = rms_scaled(residual.astype(jnp.float32), post_gain).astype(jnp.bfloat16)
    gate_share = route_weights / lax.optimization_barrier(jnp.sum(route_weights, axis=1, keepdims=True))
    sources = ROWS // ANS_DEV
    slot_rank = lax.map(rank_block, route_ids.reshape(sources, ANS_DEV * TOP_K)).reshape(ROWS * TOP_K)
    route_flat = route_ids.reshape(ROWS * TOP_K)
    entries = jnp.arange(ROWS * TOP_K, dtype=jnp.int32)
    row_owner = entries // TOP_K
    source_owner = entries // (ANS_DEV * TOP_K)
    expert_span = sources * CAPACITY
    position = route_flat * expert_span + source_owner * CAPACITY + slot_rank
    table_rows = jnp.full((EXPERTS * expert_span,), ROWS, dtype=jnp.int32).at[position].set(row_owner).reshape(EXPERTS, expert_span)
    table_gates = jnp.zeros((EXPERTS * expert_span,), dtype=jnp.float32).at[position].set(gate_share.reshape(ROWS * TOP_K)).reshape(EXPERTS, expert_span)
    padded = jnp.concatenate([normed, jnp.zeros((1, D_MODEL), dtype=jnp.bfloat16)], axis=0)

    def expert_step(accumulated, bundle):
        gate_matrix, up_matrix, down_matrix, row_index, gate_value = bundle
        inputs = padded[row_index]
        gate_part = jnp.dot(inputs, gate_matrix, preferred_element_type=jnp.float32)
        up_part = jnp.dot(inputs, up_matrix, preferred_element_type=jnp.float32)
        activated = (jax.nn.silu(gate_part) * up_part).astype(jnp.bfloat16)
        output = jnp.dot(activated, down_matrix, preferred_element_type=jnp.float32).astype(jnp.bfloat16)
        accumulated = accumulated.at[row_index].add(gate_value[:, None] * output.astype(jnp.float32))
        return (accumulated, gate_value[0])
    mixture = lax.scan(expert_step, jnp.zeros((ROWS + 1, D_MODEL), dtype=jnp.float32), (expert_gate, expert_up, expert_down, table_rows, table_gates))[0]
    return (residual.astype(jnp.float32) + mixture[:ROWS]).astype(jnp.bfloat16)
```

```python
import jax
import jax.numpy as jnp
from jax import lax
from jax.experimental import pallas as pl
from jax.experimental.pallas import tpu as pltpu
from jax.sharding import PartitionSpec as P


norm_eps = 1e-06
log2_e = 1.4426950408889634
f32, bf16 = jnp.float32, jnp.bfloat16
key_chunk = 1024
first_slots, spare_slots = 8, 4


def dot(a, b):
    return jnp.dot(a, b, preferred_element_type=f32)


def dot_t(a, b):
    return lax.dot_general(a, b, (((1,), (1,)), ((), ())), preferred_element_type=f32)


def iota(shape, dim):
    return lax.broadcasted_iota(jnp.int32, shape, dim)


def attend_kernel(
    info, q_ref, nk_ref, nv_ref, k_ref, v_ref, option_ref, qg_ref, kg_ref, out_ref, qs, acc, vext
):
    step = pl.program_id(0)
    length = info[1]
    rows, width = nk_ref.shape
    groups = q_ref.shape[1] // width
    chunk = k_ref.shape[0]
    ones = jnp.ones((width, width), bf16)

    def keys_of(raw):
        raw = raw.astype(f32)
        mean_square = dot((raw * raw).astype(bf16), ones) * (1.0 / width)
        return (raw * lax.rsqrt(mean_square + norm_eps) * kg_ref[...]).astype(bf16)

    @pl.when(step == 0)
    def _():
        vext[:, width:] = jnp.ones((chunk, width), bf16)
        gain = qg_ref[...] * (width ** (-0.5) * log2_e)
        for h in range(groups):
            raw = q_ref[:, h * width : (h + 1) * width].astype(f32)
            mean_square = jnp.mean(raw * raw, axis=-1, keepdims=True)
            qs[h * rows : (h + 1) * rows, :] = (
                raw * lax.rsqrt(mean_square + norm_eps) * gain
            ).astype(bf16)
        across = jnp.broadcast_to(option_ref[...].astype(f32), (rows, rows))
        visible = (across == across.T) & (iota((rows, rows), 1) <= iota((rows, rows), 0))
        fresh = jnp.where(visible, 1.0, 0.0)
        scores = dot_t(qs[...], keys_of(nk_ref[...]))
        fresh_values = jnp.concatenate([nv_ref[...], jnp.ones((rows, width), bf16)], axis=1)
        for h in range(groups):
            part = slice(h * rows, (h + 1) * rows)
            weights = jnp.where(fresh > 0.5, jnp.exp2(scores[part]), 0.0).astype(bf16)
            acc[part, :] = dot(weights, fresh_values)

    def visit(masked):
        vext[:, :width] = v_ref[...]
        keys = keys_of(k_ref[...])
        weights = jnp.exp2(dot_t(qs[...], keys))
        if masked:
            weights = jnp.where(iota((1, chunk), 1) < length - step * chunk, weights, 0.0)
        acc[...] += dot(weights.astype(bf16), vext[...])

    @pl.when((step + 1) * chunk <= length)
    def _():
        visit(False)

    @pl.when((step * chunk < length) & ((step + 1) * chunk > length))
    def _():
        visit(True)

    @pl.when(step == pl.num_programs(0) - 1)
    def _():
        for h in range(groups):
            part = slice(h * rows, (h + 1) * rows)
            out_ref[:, h * width : (h + 1) * width] = (
                acc[part, :width] / acc[part, width:]
            ).astype(bf16)


def attend(info, queries, new_keys, new_values, cache_keys, cache_values, option_ids, qg, kg):
    rows, width = queries.shape[0], qg.shape[1]
    key_heads = new_keys.shape[1] // width
    group_width = queries.shape[1] // key_heads
    prompt_len = cache_keys.shape[1]
    stacked = rows * group_width // width

    def live(i, info):
        return jnp.minimum(i, (info[1] - 1) // key_chunk)

    fixed = lambda i, info: (0, 0)
    of_head = lambda i, info: (0, info[0])
    cached = pl.BlockSpec((None, key_chunk, width), lambda i, info: (0, live(i, info), info[0]))
    return pl.pallas_call(
        attend_kernel,
        out_shape=jax.ShapeDtypeStruct((rows, group_width), bf16),
        grid_spec=pltpu.PrefetchScalarGridSpec(
            num_scalar_prefetch=1,
            grid=(prompt_len // key_chunk,),
            in_specs=[
                pl.BlockSpec((rows, group_width), of_head),
                pl.BlockSpec((rows, width), of_head),
                pl.BlockSpec((rows, width), of_head),
                cached,
                cached,
                pl.BlockSpec((1, rows), fixed),
                pl.BlockSpec((1, width), fixed),
                pl.BlockSpec((1, width), fixed),
            ],
            out_specs=pl.BlockSpec((rows, group_width), fixed),
            scratch_shapes=[
                pltpu.VMEM((stacked, width), bf16),
                pltpu.VMEM((stacked, 2 * width), f32),
                pltpu.VMEM((key_chunk, 2 * width), bf16),
            ],
        ),
        name="attend",
        cost_estimate=pl.CostEstimate(
            flops=8 * stacked * prompt_len * width,
            transcendentals=stacked * prompt_len,
            bytes_accessed=4 * prompt_len * width,
        ),
    )(info, queries, new_keys, new_values, cache_keys, cache_values, option_ids, qg, kg)


def project_kernel(place, x0, x1, x2, x3, own_ref, near_ref, far_ref, o0, o1, o2, o3):
    high, core = place[0], place[1]
    span, half = own_ref.shape[0], near_ref.shape[0]
    rows = x0.shape[0]
    offsets = (
        high * span,
        (1 - high) * span + core * half,
        (1 - high) * span + (1 - core) * half,
    )
    total = None
    for offset, weight in zip(offsets, (own_ref, near_ref, far_ref)):
        at = pl.ds(pl.multiple_of(offset, half), weight.shape[0])
        stacked = jnp.concatenate([x[:, at] for x in (x0, x1, x2, x3)], axis=0)
        part = dot(stacked, weight[...])
        total = part if total is None else total + part
    for i, out in enumerate((o0, o1, o2, o3)):
        out[...] = total[i * rows : (i + 1) * rows].astype(out.dtype)


def project(place, blocks, own, near, far):
    rows, span = blocks[0].shape
    model = own.shape[1]
    tile = 512
    whole = lambda a: pl.BlockSpec(a.shape, lambda i, place: (0, 0))
    column = lambda a: pl.BlockSpec((a.shape[0], tile), lambda i, place: (0, i))
    outs = [jax.ShapeDtypeStruct((rows, model), t) for t in (f32, bf16, bf16, bf16)]
    return pl.pallas_call(
        project_kernel,
        out_shape=outs,
        grid_spec=pltpu.PrefetchScalarGridSpec(
            num_scalar_prefetch=1,
            grid=(model // tile,),
            in_specs=[whole(b) for b in blocks] + [column(w) for w in (own, near, far)],
            out_specs=[column(o) for o in outs],
        ),
        name="project",
        cost_estimate=pl.CostEstimate(
            flops=8 * rows * span * model, transcendentals=0, bytes_accessed=2 * span * model
        ),
    )(place, *blocks, own, near, far)


def route_kernel(id_ref, weight_ref, send8, send4, take8, take4):
    rows, top = id_ref.shape
    experts = send8.shape[0] // first_slots
    slots = send8.shape[0]
    weights = weight_ref[...]
    share = weights / jnp.sum(weights, axis=1, keepdims=True)
    lane = iota((rows, experts), 1)
    named = jnp.zeros((rows, experts), f32)
    shares = jnp.zeros((rows, experts), f32)
    for k in range(top):
        hit = id_ref[:, k : k + 1] == lane
        named = named + jnp.where(hit, 1.0, 0.0)
        shares = shares + jnp.where(hit, share[:, k : k + 1], 0.0)
    earlier = jnp.where(iota((rows, rows), 1) < iota((rows, rows), 0), 1.0, 0.0).astype(bf16)
    rank = jnp.where(named > 0.5, dot(earlier, named.astype(bf16)), -1.0).astype(bf16)
    high = shares.astype(bf16)
    low = (shares - high.astype(f32)).astype(bf16)
    down = jnp.where(iota((slots, experts), 0) // 8 == iota((slots, experts), 1), 1.0, 0.0)
    down = down.astype(bf16)
    across = jnp.where(iota((experts, slots), 1) // 8 == iota((experts, slots), 0), 1.0, 0.0)
    across = across.astype(bf16)
    rank_down = dot_t(down, rank)
    place = iota((slots, rows), 0) % 8
    one = lambda mask: jnp.where(mask, 1.0, 0.0).astype(bf16)
    send8[...] = one(rank_down == place.astype(f32))
    spare = rank_down == (first_slots + place % 4).astype(f32)
    send4[:, :rows] = one(spare & (place < 4))
    send4[:, rows:] = one(spare & (place >= 4))
    rank_across = dot(rank, across)
    place = iota((rows, slots), 1) % 8
    hit = rank_across == place.astype(f32)
    spare = rank_across == (first_slots + place % 4).astype(f32)
    for i, part in enumerate((high, low)):
        wide = dot(part, across)
        take8[i * rows : (i + 1) * rows, :] = jnp.where(hit, wide, 0.0).astype(bf16)
        take4[i * rows : (i + 1) * rows, :] = jnp.where(spare & (place < 4), wide, 0.0).astype(bf16)
        take4[(2 + i) * rows : (3 + i) * rows, :] = jnp.where(
            spare & (place >= 4), wide, 0.0
        ).astype(bf16)


def route(route_ids, route_weights, experts):
    rows = route_ids.shape[0]
    slots = experts * 8
    shapes = ((slots, rows), (slots, 2 * rows), (2 * rows, slots), (4 * rows, slots))
    return pl.pallas_call(
        route_kernel, out_shape=[jax.ShapeDtypeStruct(s, bf16) for s in shapes], name="route"
    )(route_ids, route_weights)


def send_kernel(
    hidden_ref, own_ref, r1, r2, r3, gain_ref, send8, send4, residual_ref, out8, out4, normed, folded
):
    half = folded.shape[1]
    rows = hidden_ref.shape[0]

    @pl.when(pl.program_id(0) == 0)
    def _():
        total = own_ref[...] + r1[...].astype(f32) + r2[...].astype(f32) + r3[...].astype(f32)
        residual = (hidden_ref[...].astype(f32) + total).astype(bf16)
        residual_ref[...] = residual
        wide = residual.astype(f32)
        mean_square = jnp.mean(wide * wide, axis=-1, keepdims=True)
        scaled = (wide * lax.rsqrt(mean_square + norm_eps) * gain_ref[...]).astype(bf16)
        normed[...] = scaled
        folded[:rows, :] = scaled[:, :half]
        folded[rows:, :] = scaled[:, half:]

    out8[...] = dot(send8[...], normed[...]).astype(bf16)
    out4[...] = dot(send4[...], folded[...]).astype(bf16)


def send(hidden, own, returned, gain, send8, send4):
    rows, model = hidden.shape
    slots = send8.shape[0]
    tile = slots // 4
    whole = lambda a: pl.BlockSpec(a.shape, lambda i: (0, 0))
    line = lambda a: pl.BlockSpec((tile, a.shape[1]), lambda i: (i, 0))
    outs = [
        jax.ShapeDtypeStruct((rows, model), bf16),
        jax.ShapeDtypeStruct((slots, model), bf16),
        jax.ShapeDtypeStruct((slots, model // 2), bf16),
    ]
    return pl.pallas_call(
        send_kernel,
        out_shape=outs,
        grid=(slots // tile,),
        in_specs=[whole(a) for a in (hidden, own, *returned, gain)] + [line(send8), line(send4)],
        out_specs=[whole(outs[0]), line(outs[1]), line(outs[2])],
        scratch_shapes=[pltpu.VMEM((rows, model), bf16), pltpu.VMEM((2 * rows, model // 2), bf16)],
        name="send",
    )(hidden, own, *returned, gain, send8, send4)


def expert_of(x_parts, gate_parts, up_parts, down):
    gate = sum(dot(x, w) for x, w in zip(x_parts, gate_parts))
    up = sum(dot(x, w) for x, w in zip(x_parts, up_parts))
    activated = (gate / (1.0 + jnp.exp(-gate)) * up).astype(bf16)
    return dot(activated, down).astype(bf16)


def expert8_kernel(x_ref, gate_ref, up_ref, down_ref, out_ref):
    out_ref[...] = expert_of((x_ref[...],), (gate_ref[...],), (up_ref[...],), down_ref[...])


def expert4_kernel(x_ref, gate_ref, up_ref, down_ref, out_ref):
    slots, half = x_ref.shape
    packed = x_ref[...]
    rows = slots // 2
    row, col = iota((rows, slots), 0), iota((rows, slots), 1)
    picks = []
    for h in range(2):
        pick = col == (row // 4) * 8 + h * 4 + row % 4
        picks.append(jnp.where(pick, 1.0, 0.0).astype(bf16))
    parts = tuple(dot(pick, packed).astype(bf16) for pick in picks)
    halves = lambda w: (w[:half, :], w[half:, :])
    result = expert_of(parts, halves(gate_ref), halves(up_ref), down_ref[...])
    back = lambda pick, y: lax.dot_general(
        pick, y, (((0,), (0,)), ((), ())), preferred_element_type=f32
    )
    out_ref[...] = (back(picks[0], result[:, :half]) + back(picks[1], result[:, half:])).astype(bf16)


def expert(kernel, x, gate, up, down, tile, name):
    rows, width = x.shape
    once = lambda a: pl.BlockSpec(
        (None,) + a.shape[1:], lambda i: (0, 0, 0), pipeline_mode=pl.Buffered(1)
    )
    line = pl.BlockSpec((tile, width), lambda i: (i, 0))
    return pl.pallas_call(
        kernel,
        out_shape=jax.ShapeDtypeStruct(x.shape, bf16),
        grid=(rows // tile,),
        in_specs=[line, once(gate), once(up), once(down)],
        out_specs=line,
        name=name,
        cost_estimate=pl.CostEstimate(
            flops=6 * rows * width * gate.shape[2],
            transcendentals=rows * gate.shape[2],
            bytes_accessed=6 * gate.shape[1] * gate.shape[2],
        ),
    )(x, gate, up, down)


def take8_kernel(residual_ref, take_ref, y_ref, out_ref):
    rows = residual_ref.shape[0]
    both = dot(take_ref[...], y_ref[...])
    out_ref[...] = residual_ref[...].astype(f32) + (both[:rows] + both[rows:])


def take8(residual, take, y):
    rows, model = residual.shape
    tile = 512
    column = lambda a: pl.BlockSpec((a.shape[0], tile), lambda i: (0, i))
    return pl.pallas_call(
        take8_kernel,
        out_shape=jax.ShapeDtypeStruct((rows, model), f32),
        grid=(model // tile,),
        in_specs=[column(residual), pl.BlockSpec(take.shape, lambda i: (0, 0)), column(y)],
        out_specs=column(residual),
        name="take_first",
    )(residual, take, y)


def take4_kernel(base_ref, take_ref, y_ref, out_ref):
    rows, model = base_ref.shape
    half = model // 2
    four = dot(take_ref[...], y_ref[...])
    out_ref[:, :half] = (base_ref[:, :half] + (four[:rows] + four[rows : 2 * rows])).astype(bf16)
    out_ref[:, half:] = (
        base_ref[:, half:] + (four[2 * rows : 3 * rows] + four[3 * rows :])
    ).astype(bf16)


def take4(base, take, y):
    return pl.pallas_call(
        take4_kernel, out_shape=jax.ShapeDtypeStruct(base.shape, bf16), name="take_spare"
    )(base, take, y)


y_count, high_count, low_count, x_count, core_count = 4, 2, 2, 4, 2


def shift_y(value, by):
    pairs = [
        (y * high_count + h, (y + by) % y_count * high_count + h)
        for y in range(y_count)
        for h in range(high_count)
    ]
    return lax.ppermute(value, "expert", pairs)


def swap_core(value):
    return lax.ppermute(
        value, "attn", [(a, a ^ 1) for a in range(low_count * x_count * core_count)]
    )


def swap_high(value):
    pairs = []
    for low in range(low_count):
        for xc in range(x_count * core_count):
            for y in range(y_count):
                for h in range(high_count):
                    flat = lambda lo, hi: ((lo * x_count * core_count + xc) * y_count + y) * 2 + hi
                    pairs.append((flat(low, h), flat(1 - low, 1 - h)))
    return lax.ppermute(value, ("attn", "expert"), pairs)


def on_device(
    hidden,
    queries,
    new_keys,
    new_values,
    cache_keys,
    cache_values,
    option_ids,
    prompt_lengths,
    query_gain,
    key_gain,
    out_proj,
    post_gain,
    route_ids,
    route_weights,
    expert_gate,
    expert_up,
    expert_down,
):
    rows, model = hidden.shape
    experts = lax.axis_size("attn") * lax.axis_size("expert")
    y = lax.axis_index("expert") // high_count
    high = lax.axis_index("expert") % high_count
    core = lax.axis_index("attn") % core_count
    half = out_proj.shape[0] // 2
    near = swap_high(lax.dynamic_slice_in_dim(out_proj, core * half, half, 0))
    far = swap_core(near)

    def attend_for(by):
        info = jnp.stack([(y + by) % y_count, prompt_lengths[0]]).astype(jnp.int32)
        return attend(
            info,
            queries,
            new_keys,
            new_values,
            cache_keys,
            cache_values,
            option_ids,
            query_gain[None, :],
            key_gain[None, :],
        )

    came = {by: shift_y(attend_for(by), by) for by in (2, 1, 3)}
    mine = attend_for(0)
    place = jnp.stack([high, core]).astype(jnp.int32)
    own, p1, p2, p3 = project(place, (mine, came[1], came[2], came[3]), out_proj, near, far)
    returned = (shift_y(p2, -2), shift_y(p1, -1), shift_y(p3, -3))
    to8, to4, from8, from4 = route(route_ids, route_weights, experts)
    residual, out8, out4 = send(hidden, own, returned, post_gain[None, :], to8, to4)

    def exchange(value):
        blocks = value.reshape(experts, value.shape[0] // experts, value.shape[1])
        moved = lax.all_to_all(blocks, ("attn", "expert"), split_axis=0, concat_axis=0, tiled=True)
        return moved.reshape(value.shape)

    weights = (expert_gate, expert_up, expert_down)
    in8 = exchange(out8)
    in4 = exchange(out4)
    y8 = exchange(expert(expert8_kernel, in8, *weights, 256, "expert_first"))
    y4 = exchange(expert(expert4_kernel, in4, *weights, in4.shape[0], "expert_spare"))
    return take4(take8(residual, from8, y8), from4, y4)


def solution(mesh):
    placed = (
        P(("attn", "expert"), None),
        P(("attn", "expert"), None),
        P(("attn", "expert"), None),
        P(("attn", "expert"), None),
        P(("attn", "expert"), None, None),
        P(("attn", "expert"), None, None),
        P(("attn", "expert"), None),
        P(("attn", "expert")),
        P(),
        P(),
        P("expert", None),
        P(),
        P(("attn", "expert"), None),
        P(("attn", "expert"), None),
        P(("attn", "expert"), None, None),
        P(("attn", "expert"), None, None),
        P(("attn", "expert"), None, None),
    )
    return jax.shard_map(
        on_device,
        mesh=mesh,
        in_specs=placed,
        out_specs=P(("attn", "expert"), None),
        check_vma=False,
    )
```

```python
import jax
import jax.numpy as jnp
from jax import lax
from jax.experimental import pallas as pl
from jax.experimental.pallas import tpu as pltpu
from jax.sharding import PartitionSpec as P


norm_eps = 1e-06
log2_e = 1.4426950408889634
f32, bf16 = jnp.float32, jnp.bfloat16
key_chunk = 1024
first_slots = 8


def dot(a, b):
    return jnp.dot(a, b, preferred_element_type=f32)


def dot_t(a, b):
    return lax.dot_general(a, b, (((1,), (1,)), ((), ())), preferred_element_type=f32)


def iota(shape, dim):
    return lax.broadcasted_iota(jnp.int32, shape, dim)


def attend_kernel(
    info, q_ref, nk_ref, nv_ref, k_ref, v_ref, option_ref, qg_ref, kg_ref, out_ref, qs, keys, values
):
    length = info[1]
    rows, width = nk_ref.shape
    groups = q_ref.shape[1] // width
    cached = k_ref.shape[0]
    ones = jnp.ones((width, width), bf16)

    def keys_of(raw):
        raw = raw.astype(f32)
        mean_square = dot((raw * raw).astype(bf16), ones) * (1.0 / width)
        return (raw * lax.rsqrt(mean_square + norm_eps) * kg_ref[...]).astype(bf16)

    def prepare(first):
        part = slice(first, first + key_chunk)
        keys[part, :] = keys_of(k_ref[part, :])
        live = jnp.where(iota((key_chunk, 1), 0) + first < length, 1.0, 0.0).astype(bf16)
        values[part, :width] = v_ref[part, :] * live
        values[part, width:] = jnp.broadcast_to(live, (key_chunk, width))

    gain = qg_ref[...] * (width ** (-0.5) * log2_e)
    for h in range(groups):
        raw = q_ref[:, h * width : (h + 1) * width].astype(f32)
        mean_square = jnp.mean(raw * raw, axis=-1, keepdims=True)
        qs[h * rows : (h + 1) * rows, :] = (
            raw * lax.rsqrt(mean_square + norm_eps) * gain
        ).astype(bf16)
    keys[cached:, :] = keys_of(nk_ref[...])
    values[cached:, :width] = nv_ref[...]
    values[cached:, width:] = jnp.ones((rows, width), bf16)
    across = jnp.broadcast_to(option_ref[...].astype(f32), (rows, rows))
    visible = (across == across.T) & (iota((rows, rows), 1) <= iota((rows, rows), 0))
    block = 4 * rows
    chunks = range(0, cached, key_chunk)

    def visit(b, before):
        stacked = qs[pl.ds(b, block), :]

        def score(c):
            before(c)
            return dot_t(stacked, keys[c : c + key_chunk, :])

        scores, total = score(0), None
        for c in chunks:
            following = score(c + key_chunk) if c + key_chunk < cached else None
            part = dot(jnp.exp2(scores).astype(bf16), values[c : c + key_chunk, :])
            total = part if total is None else total + part
            scores = following
        fresh = jnp.exp2(dot_t(stacked, keys[cached:, :]))
        fresh = jnp.concatenate(
            [jnp.where(visible, fresh[r : r + rows], 0.0) for r in range(0, block, rows)], axis=0
        )
        total = total + dot(fresh.astype(bf16), values[cached:, :])
        done = (total[:, :width] / total[:, width:]).astype(bf16)
        for i in range(block // rows):
            at = pl.multiple_of((b // rows + i) * width, width)
            out_ref[:, pl.ds(at, width)] = done[i * rows : (i + 1) * rows]

    visit(0, prepare)

    @pl.loop(1, groups * rows // block)
    def _(turn):
        visit(pl.multiple_of(turn * block, block), lambda c: None)


def attend(by, info, queries, new_keys, new_values, cache_keys, cache_values, option_ids, qg, kg):
    rows, width = queries.shape[0], qg.shape[1]
    key_heads = new_keys.shape[1] // width
    group_width = queries.shape[1] // key_heads
    prompt_len = cache_keys.shape[1]
    stacked = rows * group_width // width
    head = lambda info: (info[0] + by) % key_heads
    fixed = lambda i, info: (0, 0)
    of_head = lambda i, info: (0, head(info))
    cached = pl.BlockSpec((None, prompt_len, width), lambda i, info: (0, 0, head(info)))
    return pl.pallas_call(
        attend_kernel,
        out_shape=jax.ShapeDtypeStruct((rows, group_width), bf16),
        grid_spec=pltpu.PrefetchScalarGridSpec(
            num_scalar_prefetch=1,
            grid=(1,),
            in_specs=[
                pl.BlockSpec((rows, group_width), of_head),
                pl.BlockSpec((rows, width), of_head),
                pl.BlockSpec((rows, width), of_head),
                cached,
                cached,
                pl.BlockSpec((1, rows), fixed),
                pl.BlockSpec((1, width), fixed),
                pl.BlockSpec((1, width), fixed),
            ],
            out_specs=pl.BlockSpec((rows, group_width), fixed),
            scratch_shapes=[
                pltpu.VMEM((stacked, width), bf16),
                pltpu.VMEM((prompt_len + rows, width), bf16),
                pltpu.VMEM((prompt_len + rows, 2 * width), bf16),
            ],
        ),
        name="attend",
        cost_estimate=pl.CostEstimate(
            flops=8 * stacked * prompt_len * width,
            transcendentals=stacked * prompt_len,
            bytes_accessed=4 * prompt_len * width,
        ),
    )(info, queries, new_keys, new_values, cache_keys, cache_values, option_ids, qg, kg)


def project_kernel(info, x0, x1, own_ref, near_ref, far_ref, o0, o1):
    high, core = info[2], info[3]
    span, half = own_ref.shape[0], near_ref.shape[0]
    rows = x0.shape[0]
    offsets = (
        high * span,
        (1 - high) * span + core * half,
        (1 - high) * span + (1 - core) * half,
    )
    total = None
    for offset, weight in zip(offsets, (own_ref, near_ref, far_ref)):
        at = pl.ds(pl.multiple_of(offset, half), weight.shape[0])
        part = dot(jnp.concatenate([x0[:, at], x1[:, at]], axis=0), weight[...])
        total = part if total is None else total + part
    o0[...] = total[:rows].astype(o0.dtype)
    o1[...] = total[rows:].astype(o1.dtype)


def project(info, x0, x1, own, near, far, types):
    rows, span = x0.shape
    model = own.shape[1]
    tile = 512
    whole = lambda a: pl.BlockSpec(a.shape, lambda i, info: (0, 0))
    column = lambda a: pl.BlockSpec((a.shape[0], tile), lambda i, info: (0, i))
    outs = [jax.ShapeDtypeStruct((rows, model), t) for t in types]
    return pl.pallas_call(
        project_kernel,
        out_shape=outs,
        grid_spec=pltpu.PrefetchScalarGridSpec(
            num_scalar_prefetch=1,
            grid=(model // tile,),
            in_specs=[whole(x0), whole(x1)] + [column(w) for w in (own, near, far)],
            out_specs=[column(o) for o in outs],
        ),
        name="project",
        cost_estimate=pl.CostEstimate(
            flops=4 * rows * span * model, transcendentals=0, bytes_accessed=2 * span * model
        ),
    )(info, x0, x1, own, near, far)


def named_ranks(id_ref, experts):
    rows, top = id_ref.shape
    lane = iota((rows, experts), 1)
    named = sum(jnp.where(id_ref[:, k : k + 1] == lane, 1.0, 0.0) for k in range(top))
    earlier = jnp.where(iota((rows, rows), 1) < iota((rows, rows), 0), 1.0, 0.0).astype(bf16)
    return jnp.where(named > 0.5, dot(earlier, named.astype(bf16)), -1.0).astype(bf16)


def one(mask):
    return jnp.where(mask, 1.0, 0.0).astype(bf16)


def route_send_kernel(id_ref, send8, send4):
    rows = id_ref.shape[0]
    slots = send8.shape[0]
    experts = slots // 8
    rank = named_ranks(id_ref, experts)
    down = one(iota((slots, experts), 0) // 8 == iota((slots, experts), 1))
    rank_down = dot_t(down, rank)
    place = iota((slots, rows), 0) % 8
    send8[...] = one(rank_down == place.astype(f32))
    spare = rank_down == (first_slots + place % 4).astype(f32)
    send4[:, :rows] = one(spare & (place < 4))
    send4[:, rows:] = one(spare & (place >= 4))


def route_take_kernel(id_ref, weight_ref, take8, take4):
    rows, top = id_ref.shape
    slots = take8.shape[1]
    experts = slots // 8
    rank = named_ranks(id_ref, experts)
    weights = weight_ref[...]
    share = weights / jnp.sum(weights, axis=1, keepdims=True)
    lane = iota((rows, experts), 1)
    shares = jnp.zeros((rows, experts), f32)
    for k in range(top):
        hit = id_ref[:, k : k + 1] == lane
        shares = shares + jnp.where(hit, share[:, k : k + 1], 0.0)
    high = shares.astype(bf16)
    low = (shares - high.astype(f32)).astype(bf16)
    across = one(iota((experts, slots), 1) // 8 == iota((experts, slots), 0))
    rank_across = dot(rank, across)
    place = iota((rows, slots), 1) % 8
    hit = rank_across == place.astype(f32)
    spare = rank_across == (first_slots + place % 4).astype(f32)
    for i, part in enumerate((high, low)):
        wide = dot(part, across)
        take8[i * rows : (i + 1) * rows, :] = jnp.where(hit, wide, 0.0).astype(bf16)
        take4[i * rows : (i + 1) * rows, :] = jnp.where(spare & (place < 4), wide, 0.0).astype(bf16)
        take4[(2 + i) * rows : (3 + i) * rows, :] = jnp.where(
            spare & (place >= 4), wide, 0.0
        ).astype(bf16)


def route_send(route_ids, experts):
    rows, slots = route_ids.shape[0], experts * 8
    shapes = ((slots, rows), (slots, 2 * rows))
    return pl.pallas_call(
        route_send_kernel,
        out_shape=[jax.ShapeDtypeStruct(s, bf16) for s in shapes],
        name="route_send",
    )(route_ids)


def route_take(route_ids, route_weights, experts):
    rows, slots = route_ids.shape[0], experts * 8
    shapes = ((2 * rows, slots), (4 * rows, slots))
    return pl.pallas_call(
        route_take_kernel,
        out_shape=[jax.ShapeDtypeStruct(s, bf16) for s in shapes],
        name="route_take",
    )(route_ids, route_weights)


def send_kernel(
    hidden_ref, own_ref, r1, r2, r3, gain_ref, send8, send4, residual_ref, out8, out4, normed, folded
):
    half = folded.shape[1]
    rows = hidden_ref.shape[0]

    @pl.when(pl.program_id(0) == 0)
    def _():
        total = own_ref[...] + r1[...].astype(f32) + r2[...].astype(f32) + r3[...].astype(f32)
        residual = (hidden_ref[...].astype(f32) + total).astype(bf16)
        residual_ref[...] = residual
        wide = residual.astype(f32)
        mean_square = jnp.mean(wide * wide, axis=-1, keepdims=True)
        scaled = (wide * lax.rsqrt(mean_square + norm_eps) * gain_ref[...]).astype(bf16)
        normed[...] = scaled
        folded[:rows, :] = scaled[:, :half]
        folded[rows:, :] = scaled[:, half:]

    out8[...] = dot(send8[...], normed[...]).astype(bf16)
    out4[...] = dot(send4[...], folded[...]).astype(bf16)


def send(hidden, own, returned, gain, send8, send4):
    rows, model = hidden.shape
    slots = send8.shape[0]
    tile = slots // 4
    whole = lambda a: pl.BlockSpec(a.shape, lambda i: (0, 0))
    line = lambda a: pl.BlockSpec((tile, a.shape[1]), lambda i: (i, 0))
    outs = [
        jax.ShapeDtypeStruct((rows, model), bf16),
        jax.ShapeDtypeStruct((slots, model), bf16),
        jax.ShapeDtypeStruct((slots, model // 2), bf16),
    ]
    return pl.pallas_call(
        send_kernel,
        out_shape=outs,
        grid=(slots // tile,),
        in_specs=[whole(a) for a in (hidden, own, *returned, gain)] + [line(send8), line(send4)],
        out_specs=[whole(outs[0]), line(outs[1]), line(outs[2])],
        scratch_shapes=[pltpu.VMEM((rows, model), bf16), pltpu.VMEM((2 * rows, model // 2), bf16)],
        name="send",
    )(hidden, own, *returned, gain, send8, send4)


def expert_of(x_parts, gate_parts, up_parts, down):
    gate = sum(dot(x, w) for x, w in zip(x_parts, gate_parts))
    up = sum(dot(x, w) for x, w in zip(x_parts, up_parts))
    activated = (gate / (1.0 + jnp.exp(-gate)) * up).astype(bf16)
    return dot(activated, down).astype(bf16)


def expert8_kernel(x_ref, gate_ref, up_ref, down_ref, out_ref):
    out_ref[...] = expert_of((x_ref[...],), (gate_ref[...],), (up_ref[...],), down_ref[...])


def expert4_kernel(x_ref, gate_ref, up_ref, down_ref, out_ref):
    slots, half = x_ref.shape
    packed = x_ref[...]
    rows = slots // 2
    row, col = iota((rows, slots), 0), iota((rows, slots), 1)
    picks = []
    for h in range(2):
        pick = col == (row // 4) * 8 + h * 4 + row % 4
        picks.append(jnp.where(pick, 1.0, 0.0).astype(bf16))
    parts = tuple(dot(pick, packed).astype(bf16) for pick in picks)
    halves = lambda w: (w[:half, :], w[half:, :])
    result = expert_of(parts, halves(gate_ref), halves(up_ref), down_ref[...])
    back = lambda pick, y: lax.dot_general(
        pick, y, (((0,), (0,)), ((), ())), preferred_element_type=f32
    )
    out_ref[...] = (back(picks[0], result[:, :half]) + back(picks[1], result[:, half:])).astype(bf16)


def expert(kernel, x, gate, up, down, tile):
    rows, width = x.shape
    once = lambda a: pl.BlockSpec(
        (None,) + a.shape[1:], lambda i: (0, 0, 0), pipeline_mode=pl.Buffered(1)
    )
    line = pl.BlockSpec((tile, width), lambda i: (i, 0))
    return pl.pallas_call(
        kernel,
        out_shape=jax.ShapeDtypeStruct(x.shape, bf16),
        grid=(rows // tile,),
        in_specs=[line, once(gate), once(up), once(down)],
        out_specs=line,
        cost_estimate=pl.CostEstimate(
            flops=6 * rows * width * gate.shape[2],
            transcendentals=rows * gate.shape[2],
            bytes_accessed=6 * gate.shape[1] * gate.shape[2],
        ),
    )(x, gate, up, down)


def take8_kernel(residual_ref, take_ref, y_ref, out_ref):
    rows = residual_ref.shape[0]
    both = dot(take_ref[...], y_ref[...])
    out_ref[...] = residual_ref[...].astype(f32) + (both[:rows] + both[rows:])


def take8(residual, take, y):
    rows, model = residual.shape
    tile = 512
    column = lambda a: pl.BlockSpec((a.shape[0], tile), lambda i: (0, i))
    return pl.pallas_call(
        take8_kernel,
        out_shape=jax.ShapeDtypeStruct((rows, model), f32),
        grid=(model // tile,),
        in_specs=[column(residual), pl.BlockSpec(take.shape, lambda i: (0, 0)), column(y)],
        out_specs=column(residual),
        name="take_first",
    )(residual, take, y)


def take4_kernel(base_ref, take_ref, y_ref, out_ref):
    rows, model = base_ref.shape
    half = model // 2
    tile = half // 2

    @pl.loop(0, half // tile)
    def _(i):
        first = pl.multiple_of(i * tile, tile)
        four = dot(take_ref[...], y_ref[:, pl.ds(first, tile)])
        for h in range(2):
            at = pl.ds(pl.multiple_of(first + h * half, tile), tile)
            mixed = four[2 * h * rows : (2 * h + 1) * rows] + four[(2 * h + 1) * rows :][:rows]
            out_ref[:, at] = (base_ref[:, at] + mixed).astype(bf16)


def take4(base, take, y):
    return pl.pallas_call(
        take4_kernel, out_shape=jax.ShapeDtypeStruct(base.shape, bf16), name="take_spare"
    )(base, take, y)


y_count, high_count, low_count, x_count, core_count = 4, 2, 2, 4, 2


def shift_y(value, by):
    pairs = [
        (y * high_count + h, (y + by) % y_count * high_count + h)
        for y in range(y_count)
        for h in range(high_count)
    ]
    return lax.ppermute(value, "expert", pairs)


def swap_core(value):
    return lax.ppermute(
        value, "attn", [(a, a ^ 1) for a in range(low_count * x_count * core_count)]
    )


def swap_high(value):
    pairs = []
    for low in range(low_count):
        for xc in range(x_count * core_count):
            for y in range(y_count):
                for h in range(high_count):
                    flat = lambda lo, hi: ((lo * x_count * core_count + xc) * y_count + y) * 2 + hi
                    pairs.append((flat(low, h), flat(1 - low, 1 - h)))
    return lax.ppermute(value, ("attn", "expert"), pairs)


def on_device(
    hidden,
    queries,
    new_keys,
    new_values,
    cache_keys,
    cache_values,
    option_ids,
    prompt_lengths,
    query_gain,
    key_gain,
    out_proj,
    post_gain,
    route_ids,
    route_weights,
    expert_gate,
    expert_up,
    expert_down,
):
    experts = lax.axis_size("attn") * lax.axis_size("expert")
    y = lax.axis_index("expert") // high_count
    high = lax.axis_index("expert") % high_count
    core = lax.axis_index("attn") % core_count
    half = out_proj.shape[0] // 2
    near = swap_high(lax.dynamic_slice_in_dim(out_proj, core * half, half, 0))
    info = jnp.stack([y, prompt_lengths[0], high, core]).astype(jnp.int32)

    def attend_for(by):
        return attend(
            by,
            info,
            queries,
            new_keys,
            new_values,
            cache_keys,
            cache_values,
            option_ids,
            query_gain[None, :],
            key_gain[None, :],
        )

    came2 = shift_y(attend_for(2), 2)
    came1 = shift_y(attend_for(1), 1)
    came3 = shift_y(attend_for(3), 3)
    far = swap_core(near)
    mine = attend_for(0)
    weights = (out_proj, near, far)
    p2, p1 = project(info, came2, came1, *weights, (bf16, bf16))
    r2, r1 = shift_y(p2, -2), shift_y(p1, -1)
    p3, own = project(info, came3, mine, *weights, (bf16, f32))
    returned = (r2, r1, shift_y(p3, -3))
    to8, to4 = route_send(route_ids, experts)
    from8, from4 = route_take(route_ids, route_weights, experts)
    residual, out8, out4 = send(hidden, own, returned, post_gain[None, :], to8, to4)

    def exchange(value):
        blocks = value.reshape(experts, value.shape[0] // experts, value.shape[1])
        moved = lax.all_to_all(blocks, ("attn", "expert"), split_axis=0, concat_axis=0, tiled=True)
        return moved.reshape(value.shape)

    weights = (expert_gate, expert_up, expert_down)
    in8 = exchange(out8)
    in4 = exchange(out4)
    y8 = exchange(expert(expert8_kernel, in8, *weights, 256))
    y4 = exchange(expert(expert4_kernel, in4, *weights, 256))
    return take4(take8(residual, from8, y8), from4, y4)


def solution(mesh):
    placed = (
        P(("attn", "expert"), None),
        P(("attn", "expert"), None),
        P(("attn", "expert"), None),
        P(("attn", "expert"), None),
        P(("attn", "expert"), None, None),
        P(("attn", "expert"), None, None),
        P(("attn", "expert"), None),
        P(("attn", "expert")),
        P(),
        P(),
        P("expert", None),
        P(),
        P(("attn", "expert"), None),
        P(("attn", "expert"), None),
        P(("attn", "expert"), None, None),
        P(("attn", "expert"), None, None),
        P(("attn", "expert"), None, None),
    )
    return jax.shard_map(
        on_device,
        mesh=mesh,
        in_specs=placed,
        out_specs=P(("attn", "expert"), None),
        check_vma=False,
    )
```

```python
import jax
import jax.numpy as jnp
from jax import lax
from jax.experimental import pallas as pl
from jax.experimental.pallas import tpu as pltpu
from jax.sharding import PartitionSpec as P


norm_eps = 1e-06
log2_e = 1.4426950408889634
f32, bf16 = jnp.float32, jnp.bfloat16
key_chunk = 1024
first_slots = 8


def dot(a, b):
    return jnp.dot(a, b, preferred_element_type=f32)


def dot_t(a, b):
    return lax.dot_general(a, b, (((1,), (1,)), ((), ())), preferred_element_type=f32)


def room(mib):
    return pltpu.CompilerParams(vmem_limit_bytes=mib << 20)


def held(value):
    return pltpu.with_memory_space_constraint(value, pltpu.VMEM)


def left(value):
    return pltpu.with_memory_space_constraint(value, pltpu.HBM)


in_vmem = pl.BlockSpec(memory_space=pltpu.VMEM)


def iota(shape, dim):
    return lax.broadcasted_iota(jnp.int32, shape, dim)


def attend_kernel(
    info, q_ref, nk_ref, nv_ref, k_ref, v_ref, option_ref, qg_ref, kg_ref, out_ref, qs, keys, values
):
    length = info[1]
    rows, width = nk_ref.shape
    groups = q_ref.shape[1] // width
    cached = k_ref.shape[0]
    ones = jnp.ones((width, width), bf16)

    def keys_of(raw):
        raw = raw.astype(f32)
        mean_square = dot((raw * raw).astype(bf16), ones) * (1.0 / width)
        return (raw * lax.rsqrt(mean_square + norm_eps) * kg_ref[...]).astype(bf16)

    def prepare(first):
        part = slice(first, first + key_chunk)
        keys[part, :] = keys_of(k_ref[part, :])
        live = jnp.where(iota((key_chunk, 1), 0) + first < length, 1.0, 0.0).astype(bf16)
        values[part, :width] = v_ref[part, :] * live
        values[part, width:] = jnp.broadcast_to(live, (key_chunk, width))

    gain = qg_ref[...] * (width ** (-0.5) * log2_e)
    for h in range(groups):
        raw = q_ref[:, h * width : (h + 1) * width].astype(f32)
        mean_square = jnp.mean(raw * raw, axis=-1, keepdims=True)
        qs[h * rows : (h + 1) * rows, :] = (
            raw * lax.rsqrt(mean_square + norm_eps) * gain
        ).astype(bf16)
    keys[cached:, :] = keys_of(nk_ref[...])
    values[cached:, :width] = nv_ref[...]
    values[cached:, width:] = jnp.ones((rows, width), bf16)
    across = jnp.broadcast_to(option_ref[...].astype(f32), (rows, rows))
    visible = (across == across.T) & (iota((rows, rows), 1) <= iota((rows, rows), 0))
    block = 4 * rows
    chunks = range(0, cached, key_chunk)

    def visit(b, before):
        stacked = qs[pl.ds(b, block), :]

        def score(c):
            before(c)
            return dot_t(stacked, keys[c : c + key_chunk, :])

        scores, total = score(0), None
        for c in chunks:
            following = score(c + key_chunk) if c + key_chunk < cached else None
            part = dot(jnp.exp2(scores).astype(bf16), values[c : c + key_chunk, :])
            total = part if total is None else total + part
            scores = following
        fresh = jnp.exp2(dot_t(stacked, keys[cached:, :]))
        fresh = jnp.concatenate(
            [jnp.where(visible, fresh[r : r + rows], 0.0) for r in range(0, block, rows)], axis=0
        )
        total = total + dot(fresh.astype(bf16), values[cached:, :])
        done = (total[:, :width] / total[:, width:]).astype(bf16)
        for i in range(block // rows):
            at = pl.multiple_of((b // rows + i) * width, width)
            out_ref[:, pl.ds(at, width)] = done[i * rows : (i + 1) * rows]

    visit(0, prepare)

    @pl.loop(1, groups * rows // block)
    def _(turn):
        visit(pl.multiple_of(turn * block, block), lambda c: None)


def attend(by, info, queries, new_keys, new_values, cache_keys, cache_values, option_ids, qg, kg):
    rows, width = queries.shape[0], qg.shape[1]
    key_heads = new_keys.shape[1] // width
    group_width = queries.shape[1] // key_heads
    prompt_len = cache_keys.shape[1]
    stacked = rows * group_width // width
    head = lambda info: (info[0] + by) % key_heads
    fixed = lambda i, info: (0, 0)
    of_head = lambda i, info: (0, head(info))
    cached = pl.BlockSpec((None, prompt_len, width), lambda i, info: (0, 0, head(info)))
    return pl.pallas_call(
        attend_kernel,
        out_shape=jax.ShapeDtypeStruct((rows, group_width), bf16),
        grid_spec=pltpu.PrefetchScalarGridSpec(
            num_scalar_prefetch=1,
            grid=(1,),
            in_specs=[
                pl.BlockSpec((rows, group_width), of_head),
                pl.BlockSpec((rows, width), of_head),
                pl.BlockSpec((rows, width), of_head),
                cached,
                cached,
                pl.BlockSpec((1, rows), fixed),
                pl.BlockSpec((1, width), fixed),
                pl.BlockSpec((1, width), fixed),
            ],
            out_specs=pl.BlockSpec((rows, group_width), fixed),
            scratch_shapes=[
                pltpu.VMEM((stacked, width), bf16),
                pltpu.VMEM((prompt_len + rows, width), bf16),
                pltpu.VMEM((prompt_len + rows, 2 * width), bf16),
            ],
        ),
        name="attend",
        compiler_params=room(28),
        cost_estimate=pl.CostEstimate(
            flops=8 * stacked * prompt_len * width,
            transcendentals=stacked * prompt_len,
            bytes_accessed=4 * prompt_len * width,
        ),
    )(info, queries, new_keys, new_values, cache_keys, cache_values, option_ids, qg, kg)


def project_kernel(info, x0, x1, own_ref, near_ref, far_ref, o0, o1):
    high, core = info[2], info[3]
    span, half = own_ref.shape[0], near_ref.shape[0]
    rows, model = o0.shape
    tile = model // 4
    offsets = (
        high * span,
        (1 - high) * span + core * half,
        (1 - high) * span + (1 - core) * half,
    )

    @pl.loop(0, model // tile)
    def _(i):
        column = pl.ds(pl.multiple_of(i * tile, tile), tile)
        total = None
        for offset, weight in zip(offsets, (own_ref, near_ref, far_ref)):
            at = pl.ds(pl.multiple_of(offset, half), weight.shape[0])
            part = dot(jnp.concatenate([x0[:, at], x1[:, at]], axis=0), weight[:, column])
            total = part if total is None else total + part
        o0[:, column] = total[:rows].astype(o0.dtype)
        o1[:, column] = total[rows:].astype(o1.dtype)


def project(info, x0, x1, own, near, far, types):
    rows, span = x0.shape
    model = own.shape[1]
    outs = [jax.ShapeDtypeStruct((rows, model), t) for t in types]
    return pl.pallas_call(
        project_kernel,
        out_shape=outs,
        in_specs=[pl.BlockSpec(memory_space=pltpu.SMEM)] + [in_vmem] * 5,
        out_specs=[in_vmem] * 2,
        name="project",
        compiler_params=room(24),
        cost_estimate=pl.CostEstimate(
            flops=4 * rows * span * model, transcendentals=0, bytes_accessed=2 * span * model
        ),
    )(info, *map(held, (x0, x1, own, near, far)))


def named_ranks(id_ref, experts):
    rows, top = id_ref.shape
    lane = iota((rows, experts), 1)
    named = sum(jnp.where(id_ref[:, k : k + 1] == lane, 1.0, 0.0) for k in range(top))
    earlier = jnp.where(iota((rows, rows), 1) < iota((rows, rows), 0), 1.0, 0.0).astype(bf16)
    return jnp.where(named > 0.5, dot(earlier, named.astype(bf16)), -1.0).astype(bf16)


def one(mask):
    return jnp.where(mask, 1.0, 0.0).astype(bf16)


def route_send_kernel(id_ref, send8, send4):
    rows = id_ref.shape[0]
    slots = send8.shape[0]
    experts = slots // 8
    rank = named_ranks(id_ref, experts)
    down = one(iota((slots, experts), 0) // 8 == iota((slots, experts), 1))
    rank_down = dot_t(down, rank)
    place = iota((slots, rows), 0) % 8
    send8[...] = one(rank_down == place.astype(f32))
    spare = rank_down == (first_slots + place % 4).astype(f32)
    send4[:, :rows] = one(spare & (place < 4))
    send4[:, rows:] = one(spare & (place >= 4))


def route_take_kernel(id_ref, weight_ref, take8, take4):
    rows, top = id_ref.shape
    slots = take8.shape[1]
    experts = slots // 8
    rank = named_ranks(id_ref, experts)
    weights = weight_ref[...]
    share = weights / jnp.sum(weights, axis=1, keepdims=True)
    lane = iota((rows, experts), 1)
    shares = jnp.zeros((rows, experts), f32)
    for k in range(top):
        hit = id_ref[:, k : k + 1] == lane
        shares = shares + jnp.where(hit, share[:, k : k + 1], 0.0)
    high = shares.astype(bf16)
    low = (shares - high.astype(f32)).astype(bf16)
    across = one(iota((experts, slots), 1) // 8 == iota((experts, slots), 0))
    rank_across = dot(rank, across)
    place = iota((rows, slots), 1) % 8
    hit = rank_across == place.astype(f32)
    spare = rank_across == (first_slots + place % 4).astype(f32)
    for i, part in enumerate((high, low)):
        wide = dot(part, across)
        take8[i * rows : (i + 1) * rows, :] = jnp.where(hit, wide, 0.0).astype(bf16)
        take4[i * rows : (i + 1) * rows, :] = jnp.where(spare & (place < 4), wide, 0.0).astype(bf16)
        take4[(2 + i) * rows : (3 + i) * rows, :] = jnp.where(
            spare & (place >= 4), wide, 0.0
        ).astype(bf16)


def route_send(route_ids, experts):
    rows, slots = route_ids.shape[0], experts * 8
    shapes = ((slots, rows), (slots, 2 * rows))
    return pl.pallas_call(
        route_send_kernel,
        out_shape=[jax.ShapeDtypeStruct(s, bf16) for s in shapes],
        name="route_send",
        compiler_params=room(24),
    )(route_ids)


def route_take(route_ids, route_weights, experts):
    rows, slots = route_ids.shape[0], experts * 8
    shapes = ((2 * rows, slots), (4 * rows, slots))
    return pl.pallas_call(
        route_take_kernel,
        out_shape=[jax.ShapeDtypeStruct(s, bf16) for s in shapes],
        name="route_take",
        compiler_params=room(24),
    )(route_ids, route_weights)


def send_kernel(
    hidden_ref, own_ref, r1, r2, r3, gain_ref, send8, send4, residual_ref, out_ref, normed, folded
):
    half = folded.shape[1]
    rows, model = hidden_ref.shape

    @pl.when(pl.program_id(0) == 0)
    def _():
        total = own_ref[...] + r1[...].astype(f32) + r2[...].astype(f32) + r3[...].astype(f32)
        residual = (hidden_ref[...].astype(f32) + total).astype(bf16)
        residual_ref[...] = residual
        wide = residual.astype(f32)
        mean_square = jnp.mean(wide * wide, axis=-1, keepdims=True)
        scaled = (wide * lax.rsqrt(mean_square + norm_eps) * gain_ref[...]).astype(bf16)
        normed[...] = scaled
        folded[:rows, :] = scaled[:, :half]
        folded[rows:, :] = scaled[:, half:]

    out_ref[:, :model] = dot(send8[...], normed[...]).astype(bf16)
    out_ref[:, model:] = dot(send4[...], folded[...]).astype(bf16)


def send(hidden, own, returned, gain, send8, send4):
    rows, model = hidden.shape
    slots = send8.shape[0]
    tile = slots // 4
    whole = lambda a: pl.BlockSpec(a.shape, lambda i: (0, 0))
    line = lambda a: pl.BlockSpec((tile, a.shape[1]), lambda i: (i, 0))
    outs = [
        jax.ShapeDtypeStruct((rows, model), bf16),
        jax.ShapeDtypeStruct((slots, model + model // 2), bf16),
    ]
    return pl.pallas_call(
        send_kernel,
        out_shape=outs,
        grid=(slots // tile,),
        in_specs=[in_vmem] * 6 + [line(send8), line(send4)],
        out_specs=[whole(outs[0]), line(outs[1])],
        scratch_shapes=[pltpu.VMEM((rows, model), bf16), pltpu.VMEM((2 * rows, model // 2), bf16)],
        name="send",
        compiler_params=room(28),
    )(*map(held, (hidden, own, *returned, gain)), send8, send4)


def expert_kernel(x_ref, gate, up, down, out_ref):
    slots = x_ref.shape[0]
    model = gate.shape[0]
    half = model // 2
    rows = slots // 2
    packed = x_ref[:, model:]
    row, col = iota((rows, slots), 0), iota((rows, slots), 1)
    picks = [one(col == (row // 4) * 8 + h * 4 + row % 4) for h in range(2)]
    parts = [dot(pick, packed).astype(bf16) for pick in picks]
    x = jnp.concatenate([x_ref[:, :model], jnp.concatenate(parts, axis=1)], axis=0)
    gated = dot(x, gate[...])
    activated = (gated / (1.0 + jnp.exp(-gated)) * dot(x, up[...])).astype(bf16)
    result = dot(activated, down[...]).astype(bf16)
    out_ref[:, :model] = result[:slots]
    back = lambda pick, y: lax.dot_general(
        pick, y, (((0,), (0,)), ((), ())), preferred_element_type=f32
    )
    spare = result[slots:]
    out_ref[:, model:] = (back(picks[0], spare[:, :half]) + back(picks[1], spare[:, half:])).astype(
        bf16
    )


def expert(x, gate, up, down):
    rows, width = x.shape
    tile = 256
    line = pl.BlockSpec((tile, width), lambda i: (i, 0))
    return pl.pallas_call(
        expert_kernel,
        out_shape=jax.ShapeDtypeStruct(x.shape, bf16),
        grid=(rows // tile,),
        in_specs=[line, in_vmem, in_vmem, in_vmem],
        out_specs=line,
        name="expert",
        compiler_params=room(40),
    )(x, held(gate[0]), held(up[0]), held(down[0]))


def take_kernel(residual_ref, take8_ref, take4_ref, low_ref, high_ref, spare_ref, out_ref):
    rows, model = residual_ref.shape
    tile = low_ref.shape[1]
    four = dot(take4_ref[...], spare_ref[...])
    for h, y_ref in enumerate((low_ref, high_ref)):
        both = dot(take8_ref[...], y_ref[...])
        first = pl.program_id(0) * tile + h * (model // 2)
        at = pl.ds(pl.multiple_of(first, tile), tile)
        mixed = four[2 * h * rows : (2 * h + 1) * rows] + four[(2 * h + 1) * rows :][:rows]
        out_ref[:, at] = (
            residual_ref[:, at].astype(f32) + (both[:rows] + both[rows:] + mixed)
        ).astype(bf16)


def take(residual, take8, take4, y):
    rows, model = residual.shape
    tile = 512
    turns = model // 2 // tile
    whole = lambda a: pl.BlockSpec(a.shape, lambda i: (0, 0))
    column = lambda k: pl.BlockSpec((y.shape[0], tile), lambda i: (0, k * turns + i))
    return pl.pallas_call(
        take_kernel,
        out_shape=jax.ShapeDtypeStruct((rows, model), bf16),
        grid=(turns,),
        in_specs=[whole(residual), whole(take8), whole(take4), column(0), column(1), column(2)],
        out_specs=whole(residual),
        name="take",
        compiler_params=room(28),
    )(residual, take8, take4, y, y, y)


y_count, high_count, low_count, x_count, core_count = 4, 2, 2, 4, 2


def shift_y(value, by):
    pairs = [
        (y * high_count + h, (y + by) % y_count * high_count + h)
        for y in range(y_count)
        for h in range(high_count)
    ]
    return lax.ppermute(value, "expert", pairs)


def swap_core(value):
    return lax.ppermute(
        value, "attn", [(a, a ^ 1) for a in range(low_count * x_count * core_count)]
    )


def swap_high(value):
    pairs = []
    for low in range(low_count):
        for xc in range(x_count * core_count):
            for y in range(y_count):
                for h in range(high_count):
                    flat = lambda lo, hi: ((lo * x_count * core_count + xc) * y_count + y) * 2 + hi
                    pairs.append((flat(low, h), flat(1 - low, 1 - h)))
    return lax.ppermute(value, ("attn", "expert"), pairs)


def on_device(
    hidden,
    queries,
    new_keys,
    new_values,
    cache_keys,
    cache_values,
    option_ids,
    prompt_lengths,
    query_gain,
    key_gain,
    out_proj,
    post_gain,
    route_ids,
    route_weights,
    expert_gate,
    expert_up,
    expert_down,
):
    experts = lax.axis_size("attn") * lax.axis_size("expert")
    y = lax.axis_index("expert") // high_count
    high = lax.axis_index("expert") % high_count
    core = lax.axis_index("attn") % core_count
    half = out_proj.shape[0] // 2
    near = swap_high(lax.dynamic_slice_in_dim(out_proj, core * half, half, 0))
    info = jnp.stack([y, prompt_lengths[0], high, core]).astype(jnp.int32)

    prompt = (queries, new_keys, new_values, cache_keys, cache_values, option_ids)
    prompt += (query_gain[None, :], key_gain[None, :])

    def attend_for(by, args=prompt):
        return attend(by, info, *args)

    came2 = shift_y(attend_for(2, tuple(map(left, prompt))), 2)
    came1 = shift_y(attend_for(1), 1)
    came3 = shift_y(attend_for(3), 3)
    far = swap_core(near)
    mine = attend_for(0)
    weights = (out_proj, near, far)
    p2, p1 = project(info, came2, came1, *weights, (bf16, bf16))
    r2, r1 = shift_y(p2, -2), shift_y(p1, -1)
    p3, own = project(info, came3, mine, *weights, (bf16, f32))
    returned = (r2, r1, shift_y(p3, -3))
    to8, to4 = route_send(route_ids, experts)
    from8, from4 = route_take(route_ids, route_weights, experts)
    residual, outgoing = send(hidden, own, returned, post_gain[None, :], to8, to4)

    def exchange(value):
        blocks = value.reshape(experts, value.shape[0] // experts, value.shape[1])
        moved = lax.all_to_all(blocks, ("attn", "expert"), split_axis=0, concat_axis=0, tiled=True)
        return moved.reshape(value.shape)

    mixed = exchange(expert(exchange(outgoing), expert_gate, expert_up, expert_down))
    return take(residual, from8, from4, mixed)


def solution(mesh):
    placed = (
        P(("attn", "expert"), None),
        P(("attn", "expert"), None),
        P(("attn", "expert"), None),
        P(("attn", "expert"), None),
        P(("attn", "expert"), None, None),
        P(("attn", "expert"), None, None),
        P(("attn", "expert"), None),
        P(("attn", "expert")),
        P(),
        P(),
        P("expert", None),
        P(),
        P(("attn", "expert"), None),
        P(("attn", "expert"), None),
        P(("attn", "expert"), None, None),
        P(("attn", "expert"), None, None),
        P(("attn", "expert"), None, None),
    )
    return jax.shard_map(
        on_device,
        mesh=mesh,
        in_specs=placed,
        out_specs=P(("attn", "expert"), None),
        check_vma=False,
    )
```

```python
import jax
import jax.numpy as jnp
from jax import lax
from jax.experimental import pallas as pl
from jax.experimental.pallas import tpu as pltpu
from jax.sharding import PartitionSpec as P


norm_eps = 1e-06
log2_e = 1.4426950408889634
f32, bf16 = jnp.float32, jnp.bfloat16
key_chunk = 1024
first_slots = 8


def dot(a, b):
    return jnp.dot(a, b, preferred_element_type=f32)


def dot_t(a, b):
    return lax.dot_general(a, b, (((1,), (1,)), ((), ())), preferred_element_type=f32)


def room(mib):
    return pltpu.CompilerParams(vmem_limit_bytes=mib << 20)


def held(value):
    return pltpu.with_memory_space_constraint(value, pltpu.VMEM)


def left(value):
    return pltpu.with_memory_space_constraint(value, pltpu.HBM)


in_vmem = pl.BlockSpec(memory_space=pltpu.VMEM)


def iota(shape, dim):
    return lax.broadcasted_iota(jnp.int32, shape, dim)


def attend_kernel(
    info, q_ref, nk_ref, nv_ref, k_ref, v_ref, option_ref, qg_ref, kg_ref, out_ref, qs, keys, values
):
    length = info[1]
    rows, width = nk_ref.shape
    groups = q_ref.shape[1] // width
    cached = k_ref.shape[0]
    ones = jnp.ones((width, width), bf16)

    def keys_of(raw):
        raw = raw.astype(f32)
        mean_square = dot((raw * raw).astype(bf16), ones) * (1.0 / width)
        return (raw * lax.rsqrt(mean_square + norm_eps) * kg_ref[...]).astype(bf16)

    def prepare(first):
        part = slice(first, first + key_chunk)
        keys[part, :] = keys_of(k_ref[part, :])
        live = jnp.where(iota((key_chunk, 1), 0) + first < length, 1.0, 0.0).astype(bf16)
        values[part, :width] = v_ref[part, :] * live
        values[part, width:] = jnp.broadcast_to(live, (key_chunk, width))

    gain = qg_ref[...] * (width ** (-0.5) * log2_e)
    for h in range(groups):
        raw = q_ref[:, h * width : (h + 1) * width].astype(f32)
        mean_square = jnp.mean(raw * raw, axis=-1, keepdims=True)
        qs[h * rows : (h + 1) * rows, :] = (
            raw * lax.rsqrt(mean_square + norm_eps) * gain
        ).astype(bf16)
    keys[cached:, :] = keys_of(nk_ref[...])
    values[cached:, :width] = nv_ref[...]
    values[cached:, width:] = jnp.ones((rows, width), bf16)
    across = jnp.broadcast_to(option_ref[...].astype(f32), (rows, rows))
    visible = (across == across.T) & (iota((rows, rows), 1) <= iota((rows, rows), 0))
    block = 4 * rows
    chunks = range(0, cached, key_chunk)

    def visit(b, before):
        stacked = qs[pl.ds(b, block), :]

        def score(c):
            before(c)
            return dot_t(stacked, keys[c : c + key_chunk, :])

        scores, total = score(0), None
        for c in chunks:
            following = score(c + key_chunk) if c + key_chunk < cached else None
            part = dot(jnp.exp2(scores).astype(bf16), values[c : c + key_chunk, :])
            total = part if total is None else total + part
            scores = following
        fresh = jnp.exp2(dot_t(stacked, keys[cached:, :]))
        fresh = jnp.concatenate(
            [jnp.where(visible, fresh[r : r + rows], 0.0) for r in range(0, block, rows)], axis=0
        )
        total = total + dot(fresh.astype(bf16), values[cached:, :])
        done = (total[:, :width] / total[:, width:]).astype(bf16)
        for i in range(block // rows):
            at = pl.multiple_of((b // rows + i) * width, width)
            out_ref[:, pl.ds(at, width)] = done[i * rows : (i + 1) * rows]

    visit(0, prepare)

    @pl.loop(1, groups * rows // block)
    def _(turn):
        visit(pl.multiple_of(turn * block, block), lambda c: None)


def attend(by, info, queries, new_keys, new_values, cache_keys, cache_values, option_ids, qg, kg):
    rows, width = queries.shape[0], qg.shape[1]
    key_heads = new_keys.shape[1] // width
    group_width = queries.shape[1] // key_heads
    prompt_len = cache_keys.shape[1]
    stacked = rows * group_width // width
    head = lambda info: (info[0] + by) % key_heads
    fixed = lambda i, info: (0, 0)
    of_head = lambda i, info: (0, head(info))
    cached = pl.BlockSpec((None, prompt_len, width), lambda i, info: (0, 0, head(info)))
    return pl.pallas_call(
        attend_kernel,
        out_shape=jax.ShapeDtypeStruct((rows, group_width), bf16),
        grid_spec=pltpu.PrefetchScalarGridSpec(
            num_scalar_prefetch=1,
            grid=(1,),
            in_specs=[
                pl.BlockSpec((rows, group_width), of_head),
                pl.BlockSpec((rows, width), of_head),
                pl.BlockSpec((rows, width), of_head),
                cached,
                cached,
                pl.BlockSpec((1, rows), fixed),
                pl.BlockSpec((1, width), fixed),
                pl.BlockSpec((1, width), fixed),
            ],
            out_specs=pl.BlockSpec((rows, group_width), fixed),
            scratch_shapes=[
                pltpu.VMEM((stacked, width), bf16),
                pltpu.VMEM((prompt_len + rows, width), bf16),
                pltpu.VMEM((prompt_len + rows, 2 * width), bf16),
            ],
        ),
        name="attend",
        compiler_params=room(28),
        cost_estimate=pl.CostEstimate(
            flops=8 * stacked * prompt_len * width,
            transcendentals=stacked * prompt_len,
            bytes_accessed=4 * prompt_len * width,
        ),
    )(info, queries, new_keys, new_values, cache_keys, cache_values, option_ids, qg, kg)


def project_kernel(info, *refs):
    count = (len(refs) - 3) // 2
    blocks, (own_ref, near_ref, far_ref), outs = refs[:count], refs[count:-count], refs[-count:]
    high, core = info[2], info[3]
    span, half = own_ref.shape[0], near_ref.shape[0]
    rows, model = outs[0].shape
    tile = model // 4
    offsets = (
        high * span,
        (1 - high) * span + core * half,
        (1 - high) * span + (1 - core) * half,
    )

    @pl.loop(0, model // tile)
    def _(i):
        column = pl.ds(pl.multiple_of(i * tile, tile), tile)
        total = None
        for offset, weight in zip(offsets, (own_ref, near_ref, far_ref)):
            at = pl.ds(pl.multiple_of(offset, half), weight.shape[0])
            part = dot(jnp.concatenate([x[:, at] for x in blocks], axis=0), weight[:, column])
            total = part if total is None else total + part
        for k, out in enumerate(outs):
            out[:, column] = total[k * rows : (k + 1) * rows].astype(out.dtype)


def project(info, blocks, own, near, far, out_type):
    rows, span = blocks[0].shape
    count = len(blocks)
    model = own.shape[1]
    outs = [jax.ShapeDtypeStruct((rows, model), out_type)] * count
    return pl.pallas_call(
        project_kernel,
        out_shape=outs,
        in_specs=[pl.BlockSpec(memory_space=pltpu.SMEM)] + [in_vmem] * (count + 3),
        out_specs=[in_vmem] * count,
        name="project",
        compiler_params=room(24),
        cost_estimate=pl.CostEstimate(
            flops=2 * count * rows * span * model, transcendentals=0, bytes_accessed=2 * span * model
        ),
    )(info, *map(held, (*blocks, own, near, far)))


def named_ranks(id_ref, experts):
    rows, top = id_ref.shape
    lane = iota((rows, experts), 1)
    named = sum(jnp.where(id_ref[:, k : k + 1] == lane, 1.0, 0.0) for k in range(top))
    earlier = jnp.where(iota((rows, rows), 1) < iota((rows, rows), 0), 1.0, 0.0).astype(bf16)
    return jnp.where(named > 0.5, dot(earlier, named.astype(bf16)), -1.0).astype(bf16)


def one(mask):
    return jnp.where(mask, 1.0, 0.0).astype(bf16)


def route_send_kernel(id_ref, send8, send4):
    rows = id_ref.shape[0]
    slots = send8.shape[0]
    experts = slots // 8
    rank = named_ranks(id_ref, experts)
    down = one(iota((slots, experts), 0) // 8 == iota((slots, experts), 1))
    rank_down = dot_t(down, rank)
    place = iota((slots, rows), 0) % 8
    send8[...] = one(rank_down == place.astype(f32))
    spare = rank_down == (first_slots + place % 4).astype(f32)
    send4[:, :rows] = one(spare & (place < 4))
    send4[:, rows:] = one(spare & (place >= 4))


def route_take_kernel(id_ref, weight_ref, take8, take4):
    rows, top = id_ref.shape
    slots = take8.shape[1]
    experts = slots // 8
    rank = named_ranks(id_ref, experts)
    weights = weight_ref[...]
    share = weights / jnp.sum(weights, axis=1, keepdims=True)
    lane = iota((rows, experts), 1)
    shares = jnp.zeros((rows, experts), f32)
    for k in range(top):
        hit = id_ref[:, k : k + 1] == lane
        shares = shares + jnp.where(hit, share[:, k : k + 1], 0.0)
    high = shares.astype(bf16)
    low = (shares - high.astype(f32)).astype(bf16)
    across = one(iota((experts, slots), 1) // 8 == iota((experts, slots), 0))
    rank_across = dot(rank, across)
    place = iota((rows, slots), 1) % 8
    hit = rank_across == place.astype(f32)
    spare = rank_across == (first_slots + place % 4).astype(f32)
    for i, part in enumerate((high, low)):
        wide = dot(part, across)
        take8[i * rows : (i + 1) * rows, :] = jnp.where(hit, wide, 0.0).astype(bf16)
        take4[i * rows : (i + 1) * rows, :] = jnp.where(spare & (place < 4), wide, 0.0).astype(bf16)
        take4[(2 + i) * rows : (3 + i) * rows, :] = jnp.where(
            spare & (place >= 4), wide, 0.0
        ).astype(bf16)


def route_send(route_ids, experts):
    rows, slots = route_ids.shape[0], experts * 8
    shapes = ((slots, rows), (slots, 2 * rows))
    return pl.pallas_call(
        route_send_kernel,
        out_shape=[jax.ShapeDtypeStruct(s, bf16) for s in shapes],
        name="route_send",
        compiler_params=room(24),
    )(route_ids)


def route_take(route_ids, route_weights, experts):
    rows, slots = route_ids.shape[0], experts * 8
    shapes = ((2 * rows, slots), (4 * rows, slots))
    return pl.pallas_call(
        route_take_kernel,
        out_shape=[jax.ShapeDtypeStruct(s, bf16) for s in shapes],
        name="route_take",
        compiler_params=room(24),
    )(route_ids, route_weights)


def send_kernel(
    hidden_ref, own_ref, r1, r2, r3, gain_ref, send8, send4, residual_ref, out_ref, normed, folded
):
    half = folded.shape[1]
    rows, model = hidden_ref.shape

    @pl.when(pl.program_id(0) == 0)
    def _():
        total = own_ref[...] + r1[...].astype(f32) + r2[...].astype(f32) + r3[...].astype(f32)
        residual = (hidden_ref[...].astype(f32) + total).astype(bf16)
        residual_ref[...] = residual
        wide = residual.astype(f32)
        mean_square = jnp.mean(wide * wide, axis=-1, keepdims=True)
        scaled = (wide * lax.rsqrt(mean_square + norm_eps) * gain_ref[...]).astype(bf16)
        normed[...] = scaled
        folded[:rows, :] = scaled[:, :half]
        folded[rows:, :] = scaled[:, half:]

    out_ref[:, :model] = dot(send8[...], normed[...]).astype(bf16)
    out_ref[:, model:] = dot(send4[...], folded[...]).astype(bf16)


def send(hidden, own, returned, gain, send8, send4):
    rows, model = hidden.shape
    slots = send8.shape[0]
    tile = slots // 4
    whole = lambda a: pl.BlockSpec(a.shape, lambda i: (0, 0))
    line = lambda a: pl.BlockSpec((tile, a.shape[1]), lambda i: (i, 0))
    outs = [
        jax.ShapeDtypeStruct((rows, model), bf16),
        jax.ShapeDtypeStruct((slots, model + model // 2), bf16),
    ]
    return pl.pallas_call(
        send_kernel,
        out_shape=outs,
        grid=(slots // tile,),
        in_specs=[in_vmem] * 6 + [line(send8), line(send4)],
        out_specs=[whole(outs[0]), line(outs[1])],
        scratch_shapes=[pltpu.VMEM((rows, model), bf16), pltpu.VMEM((2 * rows, model // 2), bf16)],
        name="send",
        compiler_params=room(28),
    )(*map(held, (hidden, own, *returned, gain)), send8, send4)


def expert_kernel(x_ref, gate, up, down, out_ref):
    slots = x_ref.shape[0]
    model = gate.shape[0]
    half = model // 2
    rows = slots // 2
    packed = x_ref[:, model:]
    row, col = iota((rows, slots), 0), iota((rows, slots), 1)
    picks = [one(col == (row // 4) * 8 + h * 4 + row % 4) for h in range(2)]
    parts = [dot(pick, packed).astype(bf16) for pick in picks]
    x = jnp.concatenate([x_ref[:, :model], jnp.concatenate(parts, axis=1)], axis=0)
    gated = dot(x, gate[...])
    activated = (gated / (1.0 + jnp.exp(-gated)) * dot(x, up[...])).astype(bf16)
    result = dot(activated, down[...]).astype(bf16)
    out_ref[:, :model] = result[:slots]
    back = lambda pick, y: lax.dot_general(
        pick, y, (((0,), (0,)), ((), ())), preferred_element_type=f32
    )
    spare = result[slots:]
    out_ref[:, model:] = (back(picks[0], spare[:, :half]) + back(picks[1], spare[:, half:])).astype(
        bf16
    )


def expert(x, gate, up, down):
    rows, width = x.shape
    tile = 256
    line = pl.BlockSpec((tile, width), lambda i: (i, 0))
    return pl.pallas_call(
        expert_kernel,
        out_shape=jax.ShapeDtypeStruct(x.shape, bf16),
        grid=(rows // tile,),
        in_specs=[line, in_vmem, in_vmem, in_vmem],
        out_specs=line,
        name="expert",
        compiler_params=room(40),
    )(x, held(gate[0]), held(up[0]), held(down[0]))


def take_kernel(residual_ref, take8_ref, take4_ref, low_ref, high_ref, spare_ref, out_ref):
    rows, model = residual_ref.shape
    tile = low_ref.shape[1]
    four = dot(take4_ref[...], spare_ref[...])
    for h, y_ref in enumerate((low_ref, high_ref)):
        both = dot(take8_ref[...], y_ref[...])
        first = pl.program_id(0) * tile + h * (model // 2)
        at = pl.ds(pl.multiple_of(first, tile), tile)
        mixed = four[2 * h * rows : (2 * h + 1) * rows] + four[(2 * h + 1) * rows :][:rows]
        out_ref[:, at] = (
            residual_ref[:, at].astype(f32) + (both[:rows] + both[rows:] + mixed)
        ).astype(bf16)


def take(residual, take8, take4, y):
    rows, model = residual.shape
    tile = 512
    turns = model // 2 // tile
    whole = lambda a: pl.BlockSpec(a.shape, lambda i: (0, 0))
    column = lambda k: pl.BlockSpec((y.shape[0], tile), lambda i: (0, k * turns + i))
    return pl.pallas_call(
        take_kernel,
        out_shape=jax.ShapeDtypeStruct((rows, model), bf16),
        grid=(turns,),
        in_specs=[whole(residual), whole(take8), whole(take4), column(0), column(1), column(2)],
        out_specs=whole(residual),
        name="take",
        compiler_params=room(28),
    )(residual, take8, take4, y, y, y)


y_count, high_count, low_count, x_count, core_count = 4, 2, 2, 4, 2


def shift_y(value, by):
    pairs = [
        (y * high_count + h, (y + by) % y_count * high_count + h)
        for y in range(y_count)
        for h in range(high_count)
    ]
    return lax.ppermute(value, "expert", pairs)


def swap_core(value):
    return lax.ppermute(
        value, "attn", [(a, a ^ 1) for a in range(low_count * x_count * core_count)]
    )


def swap_high(value):
    pairs = []
    for low in range(low_count):
        for xc in range(x_count * core_count):
            for y in range(y_count):
                for h in range(high_count):
                    flat = lambda lo, hi: ((lo * x_count * core_count + xc) * y_count + y) * 2 + hi
                    pairs.append((flat(low, h), flat(1 - low, 1 - h)))
    return lax.ppermute(value, ("attn", "expert"), pairs)


def on_device(
    hidden,
    queries,
    new_keys,
    new_values,
    cache_keys,
    cache_values,
    option_ids,
    prompt_lengths,
    query_gain,
    key_gain,
    out_proj,
    post_gain,
    route_ids,
    route_weights,
    expert_gate,
    expert_up,
    expert_down,
):
    experts = lax.axis_size("attn") * lax.axis_size("expert")
    y = lax.axis_index("expert") // high_count
    high = lax.axis_index("expert") % high_count
    core = lax.axis_index("attn") % core_count
    half = out_proj.shape[0] // 2
    near = swap_high(lax.dynamic_slice_in_dim(out_proj, core * half, half, 0))
    info = jnp.stack([y, prompt_lengths[0], high, core]).astype(jnp.int32)

    prompt = (queries, new_keys, new_values, cache_keys, cache_values, option_ids)
    prompt += (query_gain[None, :], key_gain[None, :])

    def attend_for(by, args=prompt):
        return attend(by, info, *args)

    came2 = shift_y(attend_for(2, tuple(map(left, prompt))), 2)
    came1 = shift_y(attend_for(1), 1)
    came3 = shift_y(attend_for(3), 3)
    far = swap_core(near)
    weights = (out_proj, near, far)
    to8, to4 = route_send(route_ids, experts)
    from8, from4 = route_take(route_ids, route_weights, experts)
    p2, p1 = project(info, (came2, came1), *weights, bf16)
    (p3,) = project(info, (came3,), *weights, bf16)
    returned = tuple(shift_y(part, -by) for by, part in ((2, p2), (1, p1), (3, p3)))
    mine = attend_for(0)
    (own,) = project(info, (mine,), *weights, f32)
    residual, outgoing = send(hidden, own, returned, post_gain[None, :], to8, to4)

    def exchange(value):
        blocks = value.reshape(experts, value.shape[0] // experts, value.shape[1])
        moved = lax.all_to_all(blocks, ("attn", "expert"), split_axis=0, concat_axis=0, tiled=True)
        return moved.reshape(value.shape)

    mixed = exchange(expert(exchange(outgoing), expert_gate, expert_up, expert_down))
    return take(residual, from8, from4, mixed)


def solution(mesh):
    placed = (
        P(("attn", "expert"), None),
        P(("attn", "expert"), None),
        P(("attn", "expert"), None),
        P(("attn", "expert"), None),
        P(("attn", "expert"), None, None),
        P(("attn", "expert"), None, None),
        P(("attn", "expert"), None),
        P(("attn", "expert")),
        P(),
        P(),
        P("expert", None),
        P(),
        P(("attn", "expert"), None),
        P(("attn", "expert"), None),
        P(("attn", "expert"), None, None),
        P(("attn", "expert"), None, None),
        P(("attn", "expert"), None, None),
    )
    return jax.shard_map(
        on_device,
        mesh=mesh,
        in_specs=placed,
        out_specs=P(("attn", "expert"), None),
        check_vma=False,
    )
```
